32 devices in a mesh: groups: 2 (over y), heads: 4 (over z), rows: 4 (over x, core).
Axes of the slice: x: 2, y: 2, z: 4, core: 2. Of those that a mesh axis runs over, the one named last changes fastest.
Arguments:
- queries: bfloat16 [512, 8192], P(('groups', 'heads')), parts along dimension 0, may hold values from -7 to 7
- kv_cache: bfloat16 [2, 4, 16384, 128], P(None, 'groups', ('heads', 'rows')), parts along dimension 1, may hold values from -7 to 7
- start_positions: int32 [4], P('groups'), parts along dimension 0, may hold values from 1024 to 1920, as said below
- residual: bfloat16 [512, 8192], P(('groups', 'heads'), 'rows'), parts along dimension 0, may hold values from -3 to 3
- out_weight: bfloat16 [8192, 8192], P('heads', 'rows'), may hold values from -2 to 2
- norm_gain: float32 [8192], P('rows'), may hold values from 0.1 to 1.9
- gate_weight: bfloat16 [8192, 14336], P('rows', 'heads'), may hold values from -0.0625 to 0.0625
- up_weight: bfloat16 [8192, 14336], P('rows', 'heads'), may hold values from -0.0625 to 0.0625
- down_weight: bfloat16 [14336, 8192], P('heads', 'rows'), may hold values from -0.046875 to 0.046875
Outputs:
- layer_out: bfloat16 [512, 8192], P(('groups', 'heads'), 'rows'), parts along dimension 0
The draws below stay inside these ranges and needn't reach their ends.
There are 2 independent parts, one for each index of `groups`. The reference program is written for one: setup_inputs(seed, part) draws one part's arguments, and reference() takes and returns one part's arrays. A program takes and returns all parts, laid end to end along the dimension named above; an argument that names none is the same for every part. Nothing has to cross between parts.
Inputs may be any that keep to these rules, and one draw needn't show every extreme that they name: Row s * 128 + t of queries is the token at position start_positions[s] + t of sequence s, and the keys and values of the new tokens already stand at those positions of kv_cache; some sequence starts at exactly 1920.
All inputs are finite; a program needn't handle non-finite values.
Results may differ from the reference program's by a relative error of at most 0.017.
Values may be sent and summed in bfloat16 or wider, within the bound.
No kernel may reach another device: no remote copies, remote signals or barrier semaphores. Data moves between devices by JAX's collectives and lax.ppermute only.
A program may use at most 128 MiB of HBM per device.

```python
import math
import jax
import jax.numpy as jnp
from jax import lax

D = 8192
QH = 64
KVH = 8
HD = 128
FF = 14336
SEQS = 2
NEW = 128
ROWS = 256
CACHE = 2048


def shared_parts(key):
    base_key = jax.random.fold_in(key, 9001)
    start_key, pick_key, common_key, sign_key = jax.random.split(base_key, 4)
    lowest = jax.random.randint(start_key, (SEQS,), CACHE // 2, CACHE - NEW + 1)
    fullest = jax.random.randint(pick_key, (), 0, SEQS)
    starts = jnp.where(jnp.arange(SEQS) == fullest, CACHE - NEW, lowest).astype(jnp.int32)
    common = jnp.clip(jax.random.normal(common_key, (SEQS * NEW, KVH, HD), jnp.float32), -3.0, 3.0)
    sign_table = (2 * jax.random.randint(sign_key, (KVH, HD), 0, 2) - 1).astype(jnp.float32)
    return (starts, common, sign_table)


def draw_start_positions(key, part):
    return shared_parts(key)[0]


def draw_queries(key, part):
    common, sign_table = shared_parts(key)[1:]
    own_key = jax.random.fold_in(key, 1)
    group_size = QH // KVH
    own_part = jnp.clip(jax.random.normal(own_key, (SEQS * NEW, QH, HD), jnp.float32), -3.0, 3.0)
    mixed = 1.5 * (0.75 * own_part + 0.66 * jnp.repeat(common, group_size, axis=1))
    return mixed.reshape(SEQS * NEW, QH * HD).astype(jnp.bfloat16)


def draw_kv_cache(key, part):
    starts, common, sign_table = shared_parts(key)
    noise_key = jax.random.fold_in(key, 2)
    full_shape = (2, SEQS, KVH, CACHE, HD)
    noise = jnp.clip(jax.random.normal(noise_key, full_shape, jnp.float32), -3.0, 3.0)
    positions = jnp.arange(CACHE)
    offset = positions[None, :] - starts[:, None]
    inside = (offset >= 0) & (offset < NEW)
    source = jnp.clip(offset, 0, NEW - 1) + (jnp.arange(SEQS) * NEW)[:, None]
    own_part = jnp.transpose(common[source], (0, 2, 1, 3))
    key_rows = jnp.where(inside[:, None, :, None], 0.75 * noise[0] + 0.66 * own_part, noise[0])
    stacked = jnp.stack([1.5 * key_rows, noise[1]])
    return stacked.reshape(2, SEQS, KVH * CACHE, HD).astype(jnp.bfloat16)


def draw_residual(key, part):
    noise_key, row_key, col_key = jax.random.split(jax.random.fold_in(key, 4), 3)
    column = jnp.arange(D, dtype=jnp.float32) / D
    noise = jnp.clip(jax.random.normal(noise_key, (ROWS, D), jnp.float32), -3.0, 3.0)
    rising = 3.0 ** (column - 1.0)
    row_scale = jnp.exp(jax.random.uniform(row_key, (ROWS, 1), jnp.float32, math.log(0.1), 0.0))
    col_scale = rising * jnp.exp(jax.random.uniform(col_key, (D,), jnp.float32, math.log(0.3), 0.0))
    return (noise * row_scale * col_scale[None, :]).astype(jnp.bfloat16)


def draw_out_weight(key, part):
    noise_key = jax.random.fold_in(key, 5)
    column = jnp.arange(D, dtype=jnp.float32) / D
    noise = jnp.clip(jax.random.normal(noise_key, (QH * HD, D), jnp.float32), -4.0, 4.0)
    rising = 3.0 ** (column - 0.5)
    return (noise * rising[None, :] * math.sqrt(64.0 / (QH * HD))).astype(jnp.bfloat16)


def block_levels(rng, shape, cuts, smallest, largest):
    level = 1.0
    for axis_at, shards_of in cuts:
        draws = jax.random.uniform(jax.random.fold_in(jax.random.fold_in(rng, 6), axis_at), (shards_of,), jnp.float32, smallest / len(cuts), largest / len(cuts))
        level = level * jnp.repeat(jnp.exp(draws), shape[axis_at] // shards_of).reshape((-1,) + (1,) * (len(shape) - 1 - axis_at))
    return level


def normal_values(key, extent, scale, reach, cuts=(), kind=jnp.bfloat16):
    array = jax.random.normal(key, extent, jnp.float32) * scale
    if len(cuts) > 0:
        array = block_levels(key, extent, cuts, -0.22, 0.18) * array
    return jnp.clip(array, min=-reach, max=reach).astype(kind)


def setup_inputs(seed: int = 0, part: int = 0) -> dict:
    keys = jax.random.split(jax.random.key(seed), 10)
    part_splits = jax.random.split(jax.random.fold_in(keys[9], part), 10)
    queries = draw_queries(jax.random.fold_in(jax.random.fold_in(keys[9], part), 71), part)
    kv_cache = draw_kv_cache(jax.random.fold_in(jax.random.fold_in(keys[9], part), 71), part)
    start_positions = draw_start_positions(jax.random.fold_in(jax.random.fold_in(keys[9], part), 71), part)
    residual = draw_residual(jax.random.fold_in(jax.random.fold_in(keys[9], part), 71), part)
    out_weight = draw_out_weight(jax.random.fold_in(keys[9], 71), part)
    norm_gain = jnp.clip(1.0 + 0.18 * jax.random.normal(keys[5], (D,), jnp.float32), 0.1, 1.9)
    gate_weight = normal_values(keys[6], (D, FF), D ** -0.5, 0.0625, ((0, 4), (1, 4)))
    up_weight = normal_values(keys[7], (D, FF), D ** -0.5, 0.0625, ((0, 4), (1, 4)))
    down_weight = normal_values(keys[8], (FF, D), FF ** -0.5, 0.046875, ((0, 4), (1, 4)))
    return dict(queries=queries, kv_cache=kv_cache, start_positions=start_positions, residual=residual, out_weight=out_weight, norm_gain=norm_gain, gate_weight=gate_weight, up_weight=up_weight, down_weight=down_weight)


def attend_sequence(query_rows, cache_keys, cache_values, last_valid):
    group_size = QH // KVH
    score_scale = 1.0 / math.sqrt(HD)
    positions = jnp.arange(CACHE, dtype=jnp.int32)
    allowed = positions[None, :] <= last_valid[:, None]
    grouped = jnp.transpose(query_rows.reshape(NEW, KVH, group_size, HD), (1, 0, 2, 3))

    def one_group(operands):
        query_group, key_group, value_group = operands
        scores = jnp.einsum('tgd,pd->gtp', query_group.astype(jnp.float32), key_group.astype(jnp.float32)) * score_scale
        scores = jnp.where(allowed[None], scores, -jnp.inf)
        row_max = lax.optimization_barrier(jnp.max(scores, axis=-1, keepdims=True))
        weights = jnp.where(allowed[None], jnp.exp(scores - row_max), 0.0)
        weight_sum = lax.optimization_barrier(jnp.sum(weights, axis=-1))
        rounded = lax.optimization_barrier(weights.astype(jnp.bfloat16)).astype(jnp.float32)
        blended = jnp.einsum('gtp,pd->tgd', rounded, value_group.astype(jnp.float32))
        return blended / jnp.transpose(weight_sum)[:, :, None]
    per_group = lax.map(one_group, (grouped, cache_keys, cache_values))
    return jnp.transpose(per_group, (1, 0, 2, 3)).reshape(NEW, QH * HD)

def reference(queries, kv_cache, start_positions, residual, out_weight, norm_gain, gate_weight, up_weight, down_weight):
    pieces = []
    for sequence in range(SEQS):
        query_rows = queries[sequence * NEW:(sequence + 1) * NEW]
        cache_keys = kv_cache[0, sequence].reshape(KVH, CACHE, HD)
        cache_values = kv_cache[1, sequence].reshape(KVH, CACHE, HD)
        last_valid = start_positions[sequence] + jnp.arange(NEW, dtype=jnp.int32)
        pieces.append(attend_sequence(query_rows, cache_keys, cache_values, last_valid))
    attended = jnp.concatenate(pieces, 0).astype(jnp.bfloat16)
    projected = jnp.dot(attended, out_weight, preferred_element_type=jnp.float32)
    resid = (residual.astype(jnp.float32) + projected).astype(jnp.bfloat16)
    resid_wide = resid.astype(jnp.float32)
    square = lax.optimization_barrier(jnp.sum(resid_wide * resid_wide, axis=1, keepdims=True))
    scaled = (resid_wide * norm_gain.astype(jnp.float32)).astype(jnp.bfloat16)
    inverse = lax.rsqrt(square / D + 1e-05)
    gate = jnp.dot(scaled, gate_weight, preferred_element_type=jnp.float32) * inverse
    up_part = jnp.dot(scaled, up_weight, preferred_element_type=jnp.float32) * inverse
    hidden = (jax.nn.silu(gate) * up_part).astype(jnp.bfloat16)
    down_part = jnp.dot(hidden, down_weight, preferred_element_type=jnp.float32)
    return (resid_wide + down_part).astype(jnp.bfloat16)
```

```python
import functools
import math

import jax
import jax.numpy as jnp
from jax import lax
from jax.experimental import pallas as pl
from jax.experimental.pallas import tpu as pltpu
from jax.sharding import PartitionSpec as P

D = 8192
QH = 64
KVH = 8
HD = 128


NEG_FILL = -1e30
EPSILON = 1e-05

CORE_SWAP = [(0, 1), (1, 0), (2, 3), (3, 2)]
CHIP_SWAP = [(0, 2), (2, 0), (1, 3), (3, 1)]
TO_CENTRE = [(0, 1), (3, 2)]
CENTRE_SWAP = [(1, 2), (2, 1)]
FROM_CENTRE = [(1, 0), (2, 3)]
VMEM_BYTES = 56 << 20

ANY = pl.BlockSpec(memory_space=pl.ANY)
VMEM = pl.BlockSpec(memory_space=pltpu.VMEM)
SMEM = pl.BlockSpec(memory_space=pltpu.SMEM)


def merged(value, axis, join):
    pieces = jax.tree.map(lambda part: lax.all_gather(part, axis), value)
    head = jax.tree.map(lambda part: part[0], pieces)
    tail = jax.tree.map(lambda part: part[1:], pieces)
    so_far, _ = lax.scan(lambda so_far, section: (join(so_far, section), None), head, tail)
    return so_far


def block_scores(query_block, cache_keys, cache_values, start_positions, first_position):
    new_count = query_block.shape[0] // cache_keys.shape[0]
    score_scale = 1.0 / math.sqrt(cache_keys.shape[2])
    positions = first_position + jnp.arange(cache_keys.shape[1], dtype=jnp.int32)
    maxima = []
    totals = []
    blends = []
    for sequence in range(cache_keys.shape[0]):
        rows_here = query_block[sequence * new_count : (sequence + 1) * new_count]
        scores = (
            jnp.einsum(
                "tkd,pd->ktp", rows_here, cache_keys[sequence], preferred_element_type=jnp.float32
            )
            * score_scale
        )
        last_valid = start_positions[sequence] + jnp.arange(new_count, dtype=jnp.int32)
        allowed = (positions[None, :] <= last_valid[:, None])[None]
        scores = jnp.where(allowed, scores, NEG_FILL)
        row_max = jnp.max(scores, axis=-1)
        weights = jnp.where(allowed, jnp.exp(scores - row_max[..., None]), 0.0)
        maxima.append(jnp.transpose(row_max))
        totals.append(jnp.transpose(jnp.sum(weights, axis=-1)))
        blends.append(
            jnp.einsum(
                "ktp,pd->tkd",
                weights.astype(jnp.bfloat16),
                cache_values[sequence],
                preferred_element_type=jnp.float32,
            )
        )
    return (jnp.concatenate(maxima, 0), jnp.concatenate(totals, 0), jnp.concatenate(blends, 0))


def merge_parts(earlier, later):
    joint = jnp.maximum(earlier[0], later[0])
    early_scale = jnp.exp(earlier[0] - joint)
    late_scale = jnp.exp(later[0] - joint)
    return (
        joint,
        earlier[1] * early_scale + later[1] * late_scale,
        earlier[2] * early_scale[..., None] + later[2] * late_scale[..., None],
    )


def general_local(
    queries,
    kv_cache,
    start_positions,
    residual,
    out_weight,
    norm_gain,
    gate_weight,
    up_weight,
    down_weight,
):
    head_count = lax.axis_size("heads")
    row_count = lax.axis_size("rows")
    head_index = lax.axis_index("heads")
    row_index = lax.axis_index("rows")
    row_block = queries.shape[0]
    total_rows = row_block * head_count
    group_size = QH // KVH
    per_group = head_count * row_count // KVH
    pos_count = kv_cache.shape[2]
    own_shard = head_index * row_count + row_index
    first_position = own_shard % per_group * pos_count
    shard_ids = jnp.arange(head_count, dtype=jnp.int32) * row_count + row_index
    shard_groups = shard_ids // per_group
    grouped = queries.reshape(row_block, KVH, group_size, HD)
    outgoing = jnp.take(grouped, shard_groups, axis=1)
    row_max, weight_sum, blended = block_scores(
        lax.all_to_all(outgoing, "heads", split_axis=1, concat_axis=0, tiled=True)[:, 0],
        kv_cache[0],
        kv_cache[1],
        start_positions,
        first_position,
    )
    got_max, got_sum, got_blend = (
        lax.all_to_all(
            row_max.reshape(head_count, row_block, group_size),
            "heads",
            split_axis=0,
            concat_axis=0,
            tiled=True,
        ),
        lax.all_to_all(
            weight_sum.reshape(head_count, row_block, group_size),
            "heads",
            split_axis=0,
            concat_axis=0,
            tiled=True,
        ),
        lax.all_to_all(
            blended.reshape(head_count, row_block, group_size, HD),
            "heads",
            split_axis=0,
            concat_axis=0,
            tiled=True,
        ),
    )
    member = (shard_groups[:, None] == jnp.arange(KVH, dtype=jnp.int32)[None, :])[:, None, :, None]
    spread_max = jnp.where(member, got_max[:, :, None, :], NEG_FILL)
    canvas_max = jnp.max(spread_max, axis=0)
    factor = jnp.where(member, jnp.exp(got_max[:, :, None, :] - canvas_max[None]), 0.0)
    canvas_sum = jnp.sum(factor * got_sum[:, :, None, :], axis=0)
    canvas_blend = jnp.einsum("srkg,srgd->rkgd", factor, got_blend, precision=lax.Precision.HIGHEST)
    joint_max, joint_sum, joint_blend = merged(
        (canvas_max, canvas_sum, canvas_blend), "rows", merge_parts
    )
    attended = (
        (joint_blend / joint_sum[..., None]).reshape(row_block, head_count, -1).astype(jnp.bfloat16)
    )
    head_rows = lax.all_to_all(attended, "heads", split_axis=1, concat_axis=0, tiled=True).reshape(
        total_rows, -1
    )
    row_start = head_index * row_block
    local_term = jnp.dot(head_rows, out_weight, preferred_element_type=jnp.float32)
    own_rows = lax.dynamic_slice_in_dim(local_term, row_start, row_block, 0) + residual.astype(
        jnp.float32
    )
    local_term = lax.dynamic_update_slice_in_dim(local_term, own_rows, row_start, 0)
    resid_all = lax.psum(local_term, "heads").astype(jnp.bfloat16)
    resid_own = lax.dynamic_slice_in_dim(resid_all, row_start, row_block, 0)
    resid_wide = resid_all.astype(jnp.float32)
    square = jnp.sum(resid_wide * resid_wide, axis=1)
    scaled = (resid_wide * norm_gain).astype(jnp.bfloat16)
    gate_part = jnp.dot(scaled, gate_weight, preferred_element_type=jnp.float32)
    up_part = jnp.dot(scaled, up_weight, preferred_element_type=jnp.float32)
    gate_sum, up_sum, square_sum = lax.psum((gate_part, up_part, square), "rows")
    inverse = lax.rsqrt(square_sum / D + EPSILON)[:, None]
    hidden = (jax.nn.silu(gate_sum * inverse) * (up_sum * inverse)).astype(jnp.bfloat16)
    down_sum = lax.psum_scatter(
        jnp.dot(hidden, down_weight, preferred_element_type=jnp.float32),
        "heads",
        scatter_dimension=0,
        tiled=True,
    )
    return (resid_own.astype(jnp.float32) + down_sum).astype(jnp.bfloat16)


def params():
    return pltpu.CompilerParams(vmem_limit_bytes=VMEM_BYTES)


def attention_kernel(info, starts, q, near, far, out):
    sequences, positions, depth = near.shape[1:]
    new_count = q.shape[0] // sequences
    heads = q.shape[1] // depth
    scale = 1.0 / math.sqrt(depth)
    core = info[2]
    shape = (heads * new_count, positions)
    token = lax.broadcasted_iota(jnp.int32, shape, 0) & (new_count - 1)
    column = lax.broadcasted_iota(jnp.int32, shape, 1)
    for s in range(sequences):
        rows = slice(s * new_count, (s + 1) * new_count)
        stacked = jnp.concatenate(
            [q[rows, k * depth : (k + 1) * depth] for k in range(heads)], axis=0
        )
        last = starts[s] + token
        scores = []
        for half, block in ((core, near), (1 - core, far)):
            raw = lax.dot_general(
                stacked, block[0, s], (((1,), (1,)), ((), ())), preferred_element_type=jnp.float32
            )
            scores.append(jnp.where(column + half * positions <= last, raw * scale, NEG_FILL))
        top = jnp.maximum(
            jnp.max(scores[0], axis=1, keepdims=True), jnp.max(scores[1], axis=1, keepdims=True)
        )
        total = 0.0
        blend = 0.0
        for half, block, score in ((core, near, scores[0]), (1 - core, far, scores[1])):
            weight = jnp.where(column + half * positions <= last, jnp.exp(score - top), 0.0)
            total += jnp.sum(weight, axis=1, keepdims=True)
            blend += jnp.dot(
                weight.astype(jnp.bfloat16), block[1, s], preferred_element_type=jnp.float32
            )
        result = (blend / total).astype(out.dtype)
        for k in range(heads):
            out[rows, k * depth : (k + 1) * depth] = result[k * new_count : (k + 1) * new_count]


def attention(info, starts, q, near, far):
    return pl.pallas_call(
        attention_kernel,
        out_shape=jax.ShapeDtypeStruct(q.shape, jnp.bfloat16),
        in_specs=[SMEM, SMEM, VMEM, VMEM, VMEM],
        out_specs=VMEM,
        compiler_params=params(),
        name="attention",
    )(info, starts, q, near, far)


def project_kernel(first, info, own, core, chip, cross, residual, w_hbm, out, w, total, sem):
    depth = own.shape[1]
    width = out.shape[1]
    pieces = (own, core, chip, cross)
    copies = []
    for j in range(4):
        row = pl.multiple_of((info[1] ^ j) * depth, depth)
        copy = pltpu.make_async_copy(
            w_hbm.at[pl.ds(row, depth), pl.ds(first, width)], w.at[j], sem.at[j]
        )
        copy.start()
        copies.append(copy)
    for j in range(4):
        copies[j].wait()
        product = jnp.dot(pieces[j][...], w[j], preferred_element_type=jnp.float32)
        if j == 0:
            total[...] = product
        else:
            total[...] += product
    block = residual.shape[0]
    mine = pl.ds(pl.multiple_of(info[0] * block, block), block)
    total[mine] += residual[:, first : first + width].astype(jnp.float32)
    for k in range(4):
        source = pl.ds(pl.multiple_of((info[4] ^ k) * block, block), block)
        out[k * block : (k + 1) * block] = total[source].astype(out.dtype)


def project(info, pieces, residual, weight, first, width):
    rows, depth = pieces[0].shape
    return pl.pallas_call(
        functools.partial(project_kernel, first),
        out_shape=jax.ShapeDtypeStruct((rows, width), jnp.bfloat16),
        in_specs=[SMEM] + [VMEM] * 5 + [ANY],
        out_specs=VMEM,
        scratch_shapes=[
            pltpu.VMEM((4, depth, width), jnp.bfloat16),
            pltpu.VMEM((rows, width), jnp.float32),
            pltpu.SemaphoreType.DMA((4,)),
        ],
        compiler_params=params(),
        name="project",
    )(info, *pieces, residual, weight)


def expand_kernel(first, step, parts, gain, *refs):
    resid = refs[:parts]
    gate_hbm, up_hbm, keep, send, square, scaled, w, sem = refs[parts:]
    count = keep.shape[1] // (2 * step)
    half = keep.shape[0]
    copies = []
    for i in range(count):
        for j, source in enumerate((gate_hbm, up_hbm)):
            copy = pltpu.make_async_copy(
                source.at[:, pl.ds(first + i * step, step)], w.at[i, j], sem.at[i, j]
            )
            copy.start()
            copies.append(copy)
    width = resid[0].shape[1]
    total = None
    for p in range(parts):
        wide = resid[p][...].astype(jnp.float32)
        piece = jnp.sum(wide * wide, axis=1, keepdims=True)
        total = piece if total is None else total + piece
        columns = slice(p * width, (p + 1) * width)
        scaled[:, columns] = (wide * gain[:, columns]).astype(jnp.bfloat16)
    square[...] = jnp.broadcast_to(total, square.shape)
    for i in range(count):
        for j in range(2):
            copies[2 * i + j].wait()
            product = jnp.dot(scaled[...], w[i, j], preferred_element_type=jnp.float32)
            product = product.astype(keep.dtype)
            columns = slice((j * count + i) * step, (j * count + i + 1) * step)
            keep[:, columns] = product[:half]
            send[:, columns] = product[half:]


def expand(resid, gain, gate_weight, up_weight, first, width, step):
    rows = resid[0].shape[0]
    parts = len(resid)
    depth = gate_weight.shape[0]
    half = jax.ShapeDtypeStruct((rows // 2, 2 * width), jnp.bfloat16)
    return pl.pallas_call(
        functools.partial(expand_kernel, first, step, parts),
        out_shape=(half, half, jax.ShapeDtypeStruct((rows, HD), jnp.float32)),
        in_specs=[VMEM] * (1 + parts) + [ANY, ANY],
        out_specs=(VMEM, VMEM, VMEM),
        scratch_shapes=[
            pltpu.VMEM((rows, depth), jnp.bfloat16),
            pltpu.VMEM((width // step, 2, depth, step), jnp.bfloat16),
            pltpu.SemaphoreType.DMA((width // step, 2)),
        ],
        compiler_params=params(),
        name="expand",
    )(gain, *resid, gate_weight, up_weight)


def contract_kernel(first, step, final, info, *refs):
    if final:
        own, chip, core, before, w_hbm, out, hidden, w, total, sem = refs
    else:
        own, chip, core, w_hbm, out, hidden, w, sem = refs
        total = out
    block = own.shape[0]
    count = own.shape[1] // step
    copies = []
    for i in range(count):
        copy = pltpu.make_async_copy(
            w_hbm.at[pl.ds(first + i * step, step)], w.at[i], sem.at[i]
        )
        copy.start()
        copies.append(copy)
    hidden[:block] = own[...]
    hidden[block : 2 * block] = chip[...]
    hidden[2 * block :] = core[...]
    for i in range(count):
        copies[i].wait()
        product = jnp.dot(
            hidden[:, i * step : (i + 1) * step], w[i], preferred_element_type=jnp.float32
        )
        if i > 0:
            total[...] += product
        elif final:
            total[...] = before[...] + product
        else:
            total[...] = product
    if final:
        for k in range(4):
            source = pl.ds(pl.multiple_of((info[4] ^ k) * block, block), block)
            out[k] = total[source].astype(out.dtype)


def contract(info, hidden, before, weight, first, step):
    own, chip, core = hidden
    block, width = own.shape
    rows = 4 * block
    columns = weight.shape[1]
    final = before is not None
    if final:
        out_shape = jax.ShapeDtypeStruct((4, block, columns), jnp.bfloat16)
    else:
        out_shape = jax.ShapeDtypeStruct((rows, columns), jnp.float32)
    scratch = [
        pltpu.VMEM((rows, width), jnp.bfloat16),
        pltpu.VMEM((width // step, step, columns), jnp.bfloat16),
    ]
    if final:
        scratch.append(pltpu.VMEM((rows, columns), jnp.float32))
    scratch.append(pltpu.SemaphoreType.DMA((width // step,)))
    arrays = [own, chip, core] + ([before] if final else [])
    return pl.pallas_call(
        functools.partial(contract_kernel, first, step, final),
        out_shape=out_shape,
        in_specs=[SMEM] + [VMEM] * len(arrays) + [ANY],
        out_specs=VMEM,
        scratch_shapes=scratch,
        compiler_params=params(),
        name="contract",
    )(info, *arrays, weight)


def wide_sum(*values):
    total = values[0].astype(jnp.float32)
    for value in values[1:]:
        total = total + value.astype(jnp.float32)
    return total


def block_local(
    queries,
    kv_cache,
    start_positions,
    residual,
    out_weight,
    norm_gain,
    gate_weight,
    up_weight,
    down_weight,
):
    z = lax.axis_index("heads")
    r = lax.axis_index("rows")
    core = r % 2
    chip = r // 2
    info = jnp.stack([z, r, core, chip, 2 * core + chip]).astype(jnp.int32)
    at_end = (z == 0) | (z == 3)
    row_block = queries.shape[0]
    far = lax.ppermute(kv_cache, "rows", CORE_SWAP)
    outgoing = lax.dynamic_index_in_dim(
        queries.reshape(row_block, 4, 4, -1), r, axis=2, keepdims=False
    )
    outgoing = jnp.transpose(outgoing, (1, 0, 2))
    q = lax.all_to_all(outgoing, "heads", split_axis=0, concat_axis=0, tiled=True)
    q = q.reshape(4 * row_block, -1)
    own = attention(info, start_positions, q, kv_cache, far)
    by_chip = lax.ppermute(own, "rows", CHIP_SWAP)
    by_core = lax.ppermute(own, "rows", CORE_SWAP)
    crossed = lax.ppermute(by_chip, "rows", CORE_SWAP)
    pieces = (own, by_core, by_chip, crossed)

    columns = out_weight.shape[1]
    chunk = columns // 4
    resid = []
    for first in range(0, columns, chunk):
        part = project(info, pieces, residual, out_weight, first, chunk)
        inward = lax.ppermute(part, "heads", TO_CENTRE)
        side = wide_sum(part, inward).astype(jnp.bfloat16)
        other = lax.ppermute(side, "heads", CENTRE_SWAP)
        both = wide_sum(side, other).astype(jnp.bfloat16)
        outward = lax.ppermute(both, "heads", FROM_CENTRE)
        resid.append(jnp.where(at_end, outward, both))

    hidden_columns = gate_weight.shape[1]
    step = 512
    cuts = [0, hidden_columns // step // 2 * step, hidden_columns]
    gain = norm_gain[None]
    inverse = None
    partial = None
    for i in range(2):
        first, width = cuts[i], cuts[i + 1] - cuts[i]
        keep, send, square = expand(resid, gain, gate_weight, up_weight, first, width, step)
        got = lax.ppermute(send, "rows", CORE_SWAP)
        if inverse is None:
            half = 2 * row_block
            square = square[:half] + lax.ppermute(square[half:], "rows", CORE_SWAP)
            square = square[:row_block] + lax.ppermute(square[row_block:], "rows", CHIP_SWAP)
            inverse = lax.rsqrt(square[:, :1] / D + EPSILON)
        passed = wide_sum(keep[row_block:], got[row_block:]).astype(jnp.bfloat16)
        arrived = lax.ppermute(passed, "rows", CHIP_SWAP)
        total = wide_sum(keep[:row_block], got[:row_block], arrived) * inverse
        hidden = (jax.nn.silu(total[:, :width]) * total[:, width:]).astype(jnp.bfloat16)
        hidden_chip = lax.ppermute(hidden, "rows", CHIP_SWAP)
        hidden_core = lax.ppermute(
            jnp.concatenate([hidden, hidden_chip], 0), "rows", CORE_SWAP
        )
        partial = contract(
            info, (hidden, hidden_chip, hidden_core), partial, down_weight, first, step
        )
    summed = wide_sum(
        *lax.all_to_all(partial, "heads", split_axis=0, concat_axis=0, tiled=True)
    )
    place = (z ^ info[4]) * row_block
    resid_own = jnp.concatenate(
        [lax.dynamic_slice_in_dim(piece, place, row_block, 0) for piece in resid], 1
    )
    return (resid_own.astype(jnp.float32) + summed).astype(jnp.bfloat16)


def solution(mesh):
    heads, rows = mesh.shape["heads"], mesh.shape["rows"]
    local = block_local if (heads, rows) == (4, 4) else general_local
    return jax.shard_map(
        local,
        mesh=mesh,
        in_specs=(
            P(("groups", "heads"), None),
            P(None, "groups", ("heads", "rows"), None),
            P("groups"),
            P(("groups", "heads"), "rows"),
            P("heads", "rows"),
            P("rows"),
            P("rows", "heads"),
            P("rows", "heads"),
            P("heads", "rows"),
        ),
        out_specs=P(("groups", "heads"), "rows"),
        check_vma=False,
    )
```
